32 devices in a mesh: gen: 4 (over y, x), dom: 4 (over z), dp: 2 (over core).
Axes of the slice: x: 2, y: 2, z: 4, core: 2. Of those that a mesh axis runs over, the one named last changes fastest.
Arguments:
- gen_hidden: bfloat16 [1024, 4096], P(('dp', 'dom'), 'gen'), parts along dimension 0, may hold values from -52 to 52
- gen_gain: float32 [8192], P('dp'), parts along dimension 0, may hold values from 0.25 to 1.75
- gen_head: bfloat16 [131072, 4096], P(('dp', 'gen', 'dom')), parts along dimension 0, may hold values from -24 to 24
- dom_hidden: bfloat16 [1024, 4096], P(('dp', 'gen'), 'dom'), parts along dimension 0, may hold values from -52 to 52
- dom_gain: float32 [8192], P('dp'), parts along dimension 0, may hold values from 0.25 to 1.75
- dom_head: bfloat16 [131072, 4096], P(('dp', 'gen', 'dom')), parts along dimension 0, may hold values from -24 to 24
- targets: int32 [1024], P('dp'), parts along dimension 0, may hold values from 0 to 65535
- doc_ids: int32 [1024], P('dp'), parts along dimension 0, may hold values from -1 to 31, as said below
Outputs:
- token_diff: float32 [1024], P(('dp', 'dom')), parts along dimension 0
- doc_score: float32 [64], P(('dp', 'dom')), parts along dimension 0
The draws below stay inside these ranges and needn't reach their ends.
There are 2 independent parts, one for each index of `dp`. The reference program is written for one: setup_inputs(seed, part) draws one part's arguments, and reference() takes and returns one part's arrays. A program takes and returns all parts, laid end to end along the dimension named above; each array names one. Nothing has to cross between parts.
Inputs may be any that keep to these rules, and one draw needn't show every extreme that they name: `doc_ids`: rows 128 * p to 128 * p + 127 form pack p. Each pack begins with rows of exactly 8 documents, numbered 8 * p onwards in order, each one row or more, and ends with padding rows marked -1. The packs fall into pairs whose document rows add up to 136, so the batch holds 272 document rows, and some pack has no padding.
All inputs are finite; a program needn't handle non-finite values.
Results may differ from the reference program's by a relative error of at most 0.0045.
Values may be sent and summed in bfloat16 or wider, within the bound.
No kernel may reach another device: no remote copies, remote signals or barrier semaphores. Data moves between devices by JAX's collectives and lax.ppermute only.
A program may use at most 128 MiB of HBM per device.

```python
import math
import jax
import jax.numpy as jnp
import numpy as np
from jax import lax

D = 4096
V = 65536
ROWS_DEV = 128
DOC_PACK = 8
ROWS = 512
DOCS = 32


def pack_layout(key):
    base = jax.random.fold_in(key, 5)
    key_order, key_length, key_pair, key_side, key_cuts = jax.random.split(base, 5)
    pack_count = ROWS // ROWS_DEV
    half_count = pack_count // 2
    order = jax.random.permutation(key_order, pack_count)
    first_len = jax.random.randint(key_length, (half_count,), DOC_PACK, ROWS_DEV + 1)
    full_pair = jax.random.randint(key_pair, (), 0, half_count)
    side_full = jax.random.randint(key_side, (), 0, 2)
    forced = jnp.where(side_full == 0, ROWS_DEV, DOC_PACK)
    first_len = jnp.where(jnp.arange(half_count) == full_pair, forced, first_len)
    second_len = ROWS_DEV + DOC_PACK - first_len
    both_len = jnp.concatenate([first_len, second_len]).astype(jnp.int32)
    lengths = jnp.zeros((pack_count,), jnp.int32).at[order].set(both_len)
    positions = jnp.arange(ROWS_DEV, dtype=jnp.int32)
    scores = jax.random.randint(key_cuts, (pack_count, ROWS_DEV), 0, 1048576) * ROWS_DEV + positions[None, :]
    usable = (positions[None, :] >= 1) & (positions[None, :] < lengths[:, None])
    scores = jnp.where(usable, scores, -1 - positions[None, :])
    cuts = lax.top_k(scores, DOC_PACK - 1)[1]
    local_doc = jnp.sum((cuts[:, None, :] <= positions[None, :, None]).astype(jnp.int32), axis=2)
    numbered = jnp.arange(pack_count, dtype=jnp.int32)[:, None] * DOC_PACK + local_doc
    doc_table = jnp.where(positions[None, :] < lengths[:, None], numbered, -1)
    return doc_table.reshape(ROWS).astype(jnp.int32)


def model_pair(key, salt_value):
    base = jax.random.fold_in(key, salt_value)
    keys = jax.random.split(base, 4)
    spread = jnp.exp(jax.random.uniform(keys[0], (V, 1), jnp.float32, 0.0, math.log(10.0)))
    trend = 1.0 + 0.2 * jnp.arange(V, dtype=jnp.float32)[:, None] / V
    weights = jax.random.truncated_normal(keys[1], -4.0, 4.0, (V, D), jnp.float32)
    weights = weights * (0.8 * spread * trend / math.sqrt(D))
    hidden = jax.random.truncated_normal(keys[3], -5.0, 5.0, (ROWS, D), jnp.float32)
    return (hidden.astype(jnp.bfloat16), weights.astype(jnp.bfloat16))


def draw_gen_hidden(key, part):
    return model_pair(key, 11)[0]


def draw_gen_head(key, part):
    return model_pair(key, 11)[1]


def draw_dom_hidden(key, part):
    return model_pair(key, 23)[0]


def draw_dom_head(key, part):
    return model_pair(key, 23)[1]


def draw_doc_ids(key, part):
    return pack_layout(key)


def with_ends(values, rng, low, top_value):
    place = [jax.random.randint(jax.random.fold_in(rng, axis), (), 0, length) for axis, length in enumerate(values.shape)]
    longest = values.shape.index(max(values.shape))
    beside = place[:longest] + [(place[longest] + 1) % values.shape[longest]] + place[longest + 1:]
    return values.at[tuple(place)].set(low).at[tuple(beside)].set(top_value)


def rank_bounds(count, lean):
    loads = [(1 << 20) // math.isqrt(standing ** lean) + 1 for standing in range(1, count + 1)]
    scale = 1 + sum(loads) // (1 << 30)
    return np.cumsum(np.array([max(1, weight // scale) for weight in loads]))


def ranked(stream_key, extent, count, lean):
    grid = rank_bounds(count, lean)
    pick = jax.random.randint(jax.random.fold_in(stream_key, 1), extent, 0, int(grid[count - 1]))
    grade = jnp.searchsorted(jnp.asarray(grid, jnp.int32), pick, side="right")
    return jax.random.permutation(jax.random.fold_in(stream_key, 2), count)[grade].astype(jnp.int32)


def setup_inputs(seed: int = 0, part: int = 0) -> dict:
    key_list = jax.random.split(jax.random.key(seed), 9)
    part_keys = jax.random.split(jax.random.fold_in(key_list[8], part), 9)
    return {
        "gen_hidden": draw_gen_hidden(jax.random.fold_in(jax.random.fold_in(key_list[8], part), 71), part),
        "gen_gain": jnp.clip(1.0 + 0.15 * jax.random.normal(part_keys[1], (D,), jnp.float32), 0.25, 1.75),
        "gen_head": draw_gen_head(jax.random.fold_in(jax.random.fold_in(key_list[8], part), 71), part),
        "dom_hidden": draw_dom_hidden(jax.random.fold_in(jax.random.fold_in(key_list[8], part), 71), part),
        "dom_gain": jnp.clip(1.0 + 0.15 * jax.random.normal(part_keys[4], (D,), jnp.float32), 0.25, 1.75),
        "dom_head": draw_dom_head(jax.random.fold_in(jax.random.fold_in(key_list[8], part), 71), part),
        "targets": with_ends(ranked(part_keys[6], (ROWS,), V, 2), jax.random.fold_in(part_keys[6], 3), 0, V - 1).astype(jnp.int32),
        "doc_ids": draw_doc_ids(jax.random.fold_in(jax.random.fold_in(key_list[8], part), 71), part),
    }


def normalize(hidden, scaling):
    values = hidden.astype(jnp.float32)
    meansq = lax.optimization_barrier(jnp.mean(values * values, axis=-1, keepdims=True))
    return (values * lax.rsqrt(meansq + 1e-05) * scaling).astype(jnp.bfloat16)

def log_probs(normed, weights, targets):
    row_blocks = normed.reshape(ROWS // ROWS_DEV, ROWS_DEV, D)
    target_blocks = targets.reshape(ROWS // ROWS_DEV, ROWS_DEV)

    def one_block(block_pair):
        row_block, wanted = block_pair
        logits = lax.dot_general(row_block, weights, (((1,), (1,)), ((), ())), preferred_element_type=jnp.float32)
        highest = lax.optimization_barrier(jnp.max(logits, axis=1, keepdims=True))
        log_total = jnp.log(lax.optimization_barrier(jnp.sum(jnp.exp(logits - highest), axis=1))) + highest[:, 0]
        picked = jnp.take_along_axis(logits, wanted[:, None].astype(jnp.int32), axis=1)[:, 0]
        return picked - log_total
    return lax.map(one_block, (row_blocks, target_blocks)).reshape(ROWS)

def reference(gen_hidden, gen_gain, gen_head, dom_hidden, dom_gain, dom_head, targets, doc_ids):
    gen_logprob = log_probs(normalize(gen_hidden, gen_gain), gen_head, targets)
    dom_logprob = log_probs(normalize(dom_hidden, dom_gain), dom_head, targets)
    is_live = doc_ids >= 0
    token_diff = jnp.where(is_live, dom_logprob - gen_logprob, jnp.zeros_like(gen_logprob))
    onehot = (doc_ids[:, None] == jnp.arange(DOCS, dtype=jnp.int32)[None, :]).astype(jnp.float32)
    doc_sums = jnp.dot(token_diff, onehot, precision=lax.Precision.HIGHEST)
    counts = lax.optimization_barrier(jnp.sum(onehot, axis=0))
    return (token_diff, doc_sums / counts)
```

```python
import functools

import jax
import jax.numpy as jnp
from jax import lax
from jax.experimental import pallas as pl
from jax.experimental.pallas import tpu as pltpu
from jax.sharding import PartitionSpec as P

DOC_PACK = 8
EPS = 1e-05
VMEM = pltpu.VMEM
SMEM = pltpu.SMEM


def whole(memory_space=VMEM):
    return pl.BlockSpec(memory_space=memory_space)


def around(block, axis):
    count = lax.axis_size(axis)
    parts = [block]
    for k in range(1, count):
        parts.append(lax.ppermute(block, axis, [(i, (i + k) % count) for i in range(count)]))
    return parts


def pack_extents(doc):
    live = jnp.where(doc >= 0, 1.0, 0.0)
    counts = jnp.sum(live, axis=1, keepdims=True)
    ahead = jnp.zeros((1, 1), jnp.float32)
    extents = []
    for p in range(doc.shape[0]):
        count = counts[p : p + 1, :]
        extents.append((count, ahead))
        ahead = ahead + count
    return extents


def slot_mask(extent, slots, rows):
    count, ahead = extent
    slot = lax.broadcasted_iota(jnp.int32, (slots, rows), 0).astype(jnp.float32)
    row = lax.broadcasted_iota(jnp.int32, (slots, rows), 1).astype(jnp.float32)
    return (slot - ahead == row) & (row < count)


def compact_kernel(index_ref, doc_ref, *refs):
    part_refs, out_ref = refs[:-1], refs[-1]
    packs = doc_ref.shape[0]
    slots = out_ref.shape[0]
    rows = doc_ref.shape[1]
    extents = pack_extents(doc_ref[...])
    mine = index_ref[0]
    total = None
    for k, part_ref in enumerate(part_refs):
        pack = lax.rem(mine - k + packs, packs)
        count = jnp.zeros((1, 1), jnp.float32)
        ahead = jnp.zeros((1, 1), jnp.float32)
        for p in range(packs):
            here = jnp.where(pack == p, 1.0, 0.0)
            count = count + extents[p][0] * here
            ahead = ahead + extents[p][1] * here
        mask = slot_mask((count, ahead), slots, rows)
        onehot = jnp.where(mask, 1.0, 0.0).astype(jnp.bfloat16)
        piece = jnp.dot(onehot, part_ref[...], preferred_element_type=jnp.float32)
        total = piece if total is None else total + piece
    out_ref[...] = total.astype(jnp.bfloat16)


def compact(parts, doc, index, slots):
    width = parts[0].shape[1]
    return pl.pallas_call(
        compact_kernel,
        out_shape=jax.ShapeDtypeStruct((slots, width), jnp.bfloat16),
        in_specs=[whole(SMEM), whole()] + [whole() for _ in parts],
        out_specs=whole(),
        cost_estimate=pl.CostEstimate(
            flops=2 * slots * width * doc.size,
            bytes_accessed=2 * width * (doc.size + slots),
            transcendentals=0,
        ),
    )(index, doc, *parts)


def stats_kernel(index_ref, doc_ref, target_ref, gain_ref, head_ref, *refs):
    part_refs = refs[:-6]
    out_ref, normed, top, total, picked, wanted = refs[-6:]
    j = pl.program_id(0)
    slots, width = normed.shape
    block_width = width // len(part_refs)
    packs, rows = doc_ref.shape
    tile = head_ref.shape[0]

    @pl.when(j == 0)
    def _():
        count = len(part_refs)
        sums = jnp.zeros((slots, 1), jnp.float32)
        for part_ref in part_refs:
            values = part_ref[...].astype(jnp.float32)
            sums = sums + jnp.sum(values * values, axis=1, keepdims=True)
        scale = lax.rsqrt(sums / width + EPS)
        for k, part_ref in enumerate(part_refs):
            block = lax.rem(index_ref[0] - k + count, count)
            at = pl.ds(pl.multiple_of(block * block_width, 128), block_width)
            values = part_ref[...].astype(jnp.float32)
            normed[:, at] = (values * scale * gain_ref[:, at]).astype(jnp.bfloat16)
        extents = pack_extents(doc_ref[...])
        ids = jnp.zeros((slots, 1), jnp.float32)
        for p in range(packs):
            mask = slot_mask(extents[p], slots, rows)
            row = (target_ref[p : p + 1, :] - index_ref[1]).astype(jnp.float32)
            ids = ids + jnp.sum(jnp.where(mask, row, 0.0), axis=1, keepdims=True)
        wanted[...] = jnp.broadcast_to(ids.astype(jnp.int32), wanted.shape)
        top[...] = jnp.full(top.shape, -jnp.inf, jnp.float32)
        total[...] = jnp.zeros(total.shape, jnp.float32)
        picked[...] = jnp.zeros(picked.shape, jnp.float32)

    logits = lax.dot_general(
        normed[...], head_ref[...], (((1,), (1,)), ((), ())), preferred_element_type=jnp.float32
    )
    columns = lax.broadcasted_iota(jnp.int32, logits.shape, 1) + j * tile
    hit = jnp.sum(jnp.where(columns == wanted[:, :1], logits, 0.0), axis=1, keepdims=True)
    former = top[:, :1]
    highest = jnp.maximum(former, jnp.max(logits, axis=1, keepdims=True))
    part = jnp.sum(jnp.exp(logits - highest), axis=1, keepdims=True)
    latest = total[:, :1] * jnp.exp(former - highest) + part
    top[...] = jnp.broadcast_to(highest, top.shape)
    total[...] = jnp.broadcast_to(latest, total.shape)
    picked[...] = picked[...] + hit

    @pl.when(j == pl.num_programs(0) - 1)
    def _():
        extents = pack_extents(doc_ref[...])
        log_total = top[:, :1] + jnp.log(total[:, :1])
        logit = picked[:, :1]
        for p in range(packs):
            mask = slot_mask(extents[p], slots, rows)
            out_ref[p, 0:1, :] = jnp.sum(jnp.where(mask, log_total, 0.0), axis=0, keepdims=True)
            out_ref[p, 1:2, :] = jnp.sum(jnp.where(mask, logit, 0.0), axis=0, keepdims=True)


def stats(parts, gain, head, doc, target, index, slots, tile):
    vocab, width = head.shape
    packs, rows = doc.shape
    column = VMEM((slots, 128), jnp.float32)
    fixed = lambda j: (0, 0)
    return pl.pallas_call(
        stats_kernel,
        grid=(vocab // tile,),
        out_shape=jax.ShapeDtypeStruct((packs, 2, rows), jnp.float32),
        in_specs=[
            whole(SMEM),
            pl.BlockSpec((packs, rows), fixed),
            pl.BlockSpec((packs, rows), fixed),
            pl.BlockSpec((1, width), fixed),
            pl.BlockSpec((tile, width), lambda j: (j, 0)),
        ]
        + [pl.BlockSpec(part.shape, fixed) for part in parts],
        out_specs=pl.BlockSpec((packs, 2, rows), lambda j: (0, 0, 0)),
        scratch_shapes=[
            VMEM((slots, width), jnp.bfloat16),
            column,
            column,
            column,
            VMEM((slots, 128), jnp.int32),
        ],
        compiler_params=pltpu.CompilerParams(vmem_limit_bytes=40 * 1024 * 1024),
        cost_estimate=pl.CostEstimate(
            flops=2 * slots * width * vocab,
            bytes_accessed=2 * width * (vocab + slots),
            transcendentals=slots * vocab,
        ),
    )(index, doc, target, gain.reshape(1, width), head, *parts)


def finish_kernel(index_ref, doc_ref, all_ref, token_ref, score_ref):
    pack = index_ref[0]
    members = all_ref.shape[0]
    both = all_ref[...]

    def log_prob(at):
        logs = [both[i, at : at + 1, :] for i in range(members)]
        highest = functools.reduce(jnp.maximum, logs)
        summed = functools.reduce(jnp.add, [jnp.exp(one - highest) for one in logs])
        logit = functools.reduce(jnp.add, [both[i, at + 1 : at + 2, :] for i in range(members)])
        return logit - (highest + jnp.log(summed))

    ids = doc_ref[pl.ds(pack, 1), :]
    diff = jnp.where(ids >= 0, log_prob(2) - log_prob(0), 0.0)
    token_ref[...] = diff
    rows = ids.shape[1]
    number = lax.broadcasted_iota(jnp.int32, (DOC_PACK, rows), 0) + pack * DOC_PACK
    mine = number == ids
    sums = jnp.sum(jnp.where(mine, diff, 0.0), axis=1, keepdims=True)
    counts = jnp.sum(jnp.where(mine, 1.0, 0.0), axis=1, keepdims=True)
    score = sums / counts
    row = lax.broadcasted_iota(jnp.int32, (DOC_PACK, DOC_PACK), 0)
    column = lax.broadcasted_iota(jnp.int32, (DOC_PACK, DOC_PACK), 1)
    score_ref[...] = jnp.sum(jnp.where(row == column, score, 0.0), axis=0, keepdims=True)


def finish(gathered, doc, index):
    rows = doc.shape[1]
    token, score = pl.pallas_call(
        finish_kernel,
        out_shape=(
            jax.ShapeDtypeStruct((1, rows), jnp.float32),
            jax.ShapeDtypeStruct((1, DOC_PACK), jnp.float32),
        ),
        in_specs=[whole(SMEM), whole(), whole()],
        out_specs=(whole(), whole()),
    )(index, doc, gathered)
    return token.reshape(rows), score.reshape(DOC_PACK)


def per_device(gen_hidden, gen_gain, gen_head, dom_hidden, dom_gain, dom_head, targets, doc_ids):
    rows = gen_hidden.shape[0]
    gen_count = lax.axis_size("gen")
    dom_count = lax.axis_size("dom")
    gen_index = lax.axis_index("gen")
    dom_index = lax.axis_index("dom")
    first = (gen_index * dom_count + dom_index) * gen_head.shape[0]
    gen_at = jnp.stack([gen_index, first]).astype(jnp.int32)
    dom_at = jnp.stack([dom_index, first]).astype(jnp.int32)
    doc = doc_ids.reshape(dom_count, rows)
    target = targets.reshape(dom_count, rows)
    slots = dom_count // 2 * (rows + DOC_PACK)

    dom_first = around(dom_hidden, "gen")
    gen_first = around(gen_hidden, "dom")
    dom_rows = compact(dom_first, doc, gen_at, slots)
    dom_parts = around(dom_rows, "dom")
    gen_rows = compact(gen_first, doc, dom_at, slots)
    gen_parts = around(gen_rows, "gen")

    tile = min(512, gen_head.shape[0])
    gen_stats = stats(gen_parts, gen_gain, gen_head, doc, target, gen_at, slots, tile)
    dom_stats = stats(dom_parts, dom_gain, dom_head, doc, target, dom_at, slots, tile)
    both = jnp.concatenate([gen_stats, dom_stats], axis=1)
    sent = jnp.broadcast_to(both[None], (gen_count,) + both.shape)
    sent = sent.reshape((gen_count * dom_count,) + both.shape[1:])
    gathered = lax.all_to_all(sent, ("gen", "dom"), 0, 0)
    return finish(gathered, doc, dom_at)


def solution(mesh):
    in_specs = (
        P(("dp", "dom"), "gen"),
        P("dp"),
        P(("dp", "gen", "dom"), None),
        P(("dp", "gen"), "dom"),
        P("dp"),
        P(("dp", "gen", "dom"), None),
        P("dp"),
        P("dp"),
    )
    out_specs = (P(("dp", "dom")), P(("dp", "dom")))
    return jax.shard_map(
        per_device, mesh=mesh, in_specs=in_specs, out_specs=out_specs, check_vma=False
    )
```

```python
import functools

import jax
import jax.numpy as jnp
from jax import lax
from jax.experimental import pallas as pl
from jax.experimental.pallas import tpu as pltpu
from jax.sharding import PartitionSpec as P


DOC_PACK = 8
EPS = 1e-05
VMEM = pltpu.VMEM
SMEM = pltpu.SMEM


def whole(memory_space=VMEM):
    return pl.BlockSpec(memory_space=memory_space)


def around(block, axis):
    count = lax.axis_size(axis)
    parts = [block]
    for k in range(1, count):
        parts.append(lax.ppermute(block, axis, [(i, (i + k) % count) for i in range(count)]))
    return parts


def column_of(row):
    count = row.shape[1]
    here = lax.broadcasted_iota(jnp.int32, (count, count), 0)
    there = lax.broadcasted_iota(jnp.int32, (count, count), 1)
    return jnp.sum(jnp.where(here == there, row, 0.0), axis=1, keepdims=True)


def row_of(column):
    count = column.shape[0]
    here = lax.broadcasted_iota(jnp.int32, (count, count), 0)
    there = lax.broadcasted_iota(jnp.int32, (count, count), 1)
    return jnp.sum(jnp.where(here == there, column, 0.0), axis=0, keepdims=True)


def pack_extents(doc):
    live = jnp.where(doc >= 0, 1.0, 0.0)
    counts = jnp.sum(live, axis=1, keepdims=True)
    ahead = jnp.zeros((1, 1), jnp.float32)
    extents = []
    for p in range(doc.shape[0]):
        count = counts[p : p + 1, :]
        extents.append((count, ahead))
        ahead = ahead + count
    return extents


def slot_mask(extent, slots, rows):
    count, ahead = extent
    slot = lax.broadcasted_iota(jnp.int32, (slots, rows), 0).astype(jnp.float32)
    row = lax.broadcasted_iota(jnp.int32, (slots, rows), 1).astype(jnp.float32)
    return (slot - ahead == row) & (row < count)


def compact_kernel(index_ref, doc_ref, *refs):
    part_refs, out_ref, square_ref = refs[:-2], refs[-2], refs[-1]
    packs = doc_ref.shape[0]
    slots = out_ref.shape[0]
    rows = doc_ref.shape[1]
    extents = pack_extents(doc_ref[...])
    mine = index_ref[0]
    total = None
    for k, part_ref in enumerate(part_refs):
        pack = lax.rem(mine - k + packs, packs)
        count = jnp.zeros((1, 1), jnp.float32)
        ahead = jnp.zeros((1, 1), jnp.float32)
        for p in range(packs):
            here = jnp.where(pack == p, 1.0, 0.0)
            count = count + extents[p][0] * here
            ahead = ahead + extents[p][1] * here
        mask = slot_mask((count, ahead), slots, rows)
        onehot = jnp.where(mask, 1.0, 0.0).astype(jnp.bfloat16)
        piece = jnp.dot(onehot, part_ref[...], preferred_element_type=jnp.float32)
        total = piece if total is None else total + piece
    out_ref[...] = total.astype(jnp.bfloat16)
    squares = jnp.sum(total * total, axis=1, keepdims=True)
    square_ref[...] = jnp.broadcast_to(row_of(squares), square_ref.shape)


def compact(parts, doc, index, slots):
    width = parts[0].shape[1]
    return pl.pallas_call(
        compact_kernel,
        out_shape=(
            jax.ShapeDtypeStruct((slots, width), jnp.bfloat16),
            jax.ShapeDtypeStruct((8, slots), jnp.float32),
        ),
        in_specs=[whole(SMEM), whole()] + [whole() for _ in parts],
        out_specs=(whole(), whole()),
        compiler_params=pltpu.CompilerParams(vmem_limit_bytes=16 * 1024 * 1024),
        cost_estimate=pl.CostEstimate(
            flops=2 * slots * width * doc.size,
            bytes_accessed=2 * width * (doc.size + slots),
            transcendentals=0,
        ),
    )(index, doc, *parts)


def blocks_kernel(setup, index_ref, doc_ref, target_ref, gain_ref, head_ref, *refs):
    block_count, square_count, holds, closing, buffers = setup
    refs = list(refs)
    take = lambda n: [refs.pop(0) for _ in range(n)]
    part_refs = take(block_count)
    square_refs = take(square_count)
    held_ref = take(1)[0] if holds else None
    out_ref, normed, tiles, sems = take(4)
    slots = normed.shape[0]
    block_width = normed.shape[1] // block_count
    width = head_ref.shape[1]
    tile = tiles.shape[1]
    packs, rows = doc_ref.shape
    j = pl.program_id(0)
    steps = pl.num_programs(0)

    def copy(step, k):
        slot = lax.rem(step, buffers)
        number = pl.multiple_of(index_ref[k] * block_width, block_width)
        return pltpu.make_async_copy(
            head_ref.at[pl.ds(step * tile, tile), pl.ds(number, block_width)],
            tiles.at[slot, :, pl.ds(k * block_width, block_width)],
            sems.at[slot, k],
        )

    def begin(step):
        for k in range(block_count):
            copy(step, k).start()

    @pl.when(j == 0)
    def _():
        begin(0)
        for step in range(1, buffers - 1):
            pl.when(step < steps)(functools.partial(begin, step))

    @pl.when(j + buffers - 1 < steps)
    def _():
        begin(j + buffers - 1)

    @pl.when(j == 0)
    def _():
        if square_count:
            sums = column_of(functools.reduce(jnp.add, [ref[0:1, :] for ref in square_refs]))
        else:
            sums = jnp.zeros((slots, 1), jnp.float32)
            for part_ref in part_refs:
                values = part_ref[...].astype(jnp.float32)
                sums = sums + jnp.sum(values * values, axis=1, keepdims=True)
        scale = lax.rsqrt(sums / width + EPS)
        for k, part_ref in enumerate(part_refs):
            number = pl.multiple_of(index_ref[k] * block_width, block_width)
            gain = gain_ref[:, pl.ds(number, block_width)]
            values = part_ref[...].astype(jnp.float32)
            at = slice(k * block_width, (k + 1) * block_width)
            normed[:, at] = (values * scale * gain).astype(jnp.bfloat16)

    for k in range(block_count):
        copy(j, k).wait()
    logits = lax.dot_general(
        normed[...],
        tiles[lax.rem(j, buffers)],
        (((1,), (1,)), ((), ())),
        preferred_element_type=jnp.float32,
    )
    across = pl.ds(pl.multiple_of(j * tile, tile), tile)
    if holds:
        logits = logits + held_ref[:, across]
    if not closing:
        out_ref[:, across] = logits
        return
    top, total, picked, wanted = refs

    @pl.when(j == 0)
    def _():
        extents = pack_extents(doc_ref[...])
        ids = jnp.zeros((slots, 1), jnp.float32)
        for p in range(packs):
            mask = slot_mask(extents[p], slots, rows)
            row = (target_ref[p : p + 1, :] - index_ref[block_count]).astype(jnp.float32)
            ids = ids + jnp.sum(jnp.where(mask, row, 0.0), axis=1, keepdims=True)
        wanted[...] = jnp.broadcast_to(ids.astype(jnp.int32), wanted.shape)
        top[...] = jnp.full(top.shape, -jnp.inf, jnp.float32)
        total[...] = jnp.zeros(total.shape, jnp.float32)
        picked[...] = jnp.zeros(picked.shape, jnp.float32)

    columns = lax.broadcasted_iota(jnp.int32, logits.shape, 1)
    here = wanted[:, :1] - j * tile
    hit = jnp.sum(jnp.where(columns == here, logits, 0.0), axis=1, keepdims=True)
    former = top[:, :1]
    highest = jnp.maximum(former, jnp.max(logits, axis=1, keepdims=True))
    part = jnp.sum(jnp.exp(logits - highest), axis=1, keepdims=True)
    latest = total[:, :1] * jnp.exp(former - highest) + part
    top[...] = jnp.broadcast_to(highest, top.shape)
    total[...] = jnp.broadcast_to(latest, total.shape)
    picked[...] = picked[...] + hit

    @pl.when(j == steps - 1)
    def _():
        extents = pack_extents(doc_ref[...])
        log_total = top[:, :1] + jnp.log(total[:, :1])
        logit = picked[:, :1]
        for p in range(packs):
            mask = slot_mask(extents[p], slots, rows)
            out_ref[p, 0:1, :] = jnp.sum(jnp.where(mask, log_total, 0.0), axis=0, keepdims=True)
            out_ref[p, 1:2, :] = jnp.sum(jnp.where(mask, logit, 0.0), axis=0, keepdims=True)


def blocks(parts, numbers, first, squares, held, gain, head, doc, target, tile, closing):
    slots, block_width = parts[0].shape
    vocab, width = head.shape
    packs, rows = doc.shape
    tile = min(tile, vocab)
    count = len(parts)
    buffers = 3
    column = VMEM((slots, 128), jnp.float32)
    scratch = [
        VMEM((slots, count * block_width), jnp.bfloat16),
        VMEM((buffers, tile, count * block_width), jnp.bfloat16),
        pltpu.SemaphoreType.DMA((buffers, count)),
    ]
    if closing:
        out_shape = jax.ShapeDtypeStruct((packs, 2, rows), jnp.float32)
        scratch += [column, column, column, VMEM((slots, 128), jnp.int32)]
    else:
        out_shape = jax.ShapeDtypeStruct((slots, vocab), jnp.float32)
    operands = [doc, target, gain.reshape(1, width), head] + list(parts) + list(squares)
    in_specs = [whole(SMEM), whole(), whole(), whole(), whole(pl.ANY)]
    in_specs += [whole() for _ in operands[4:]]
    if held is not None:
        operands.append(held)
        in_specs.append(whole())
    index = jnp.stack(list(numbers) + [first]).astype(jnp.int32)
    setup = (count, len(squares), held is not None, closing, buffers)
    return pl.pallas_call(
        functools.partial(blocks_kernel, setup),
        grid=(vocab // tile,),
        in_specs=in_specs,
        out_specs=whole(),
        out_shape=out_shape,
        scratch_shapes=scratch,
        compiler_params=pltpu.CompilerParams(vmem_limit_bytes=32 * 1024 * 1024),
        cost_estimate=pl.CostEstimate(
            flops=2 * slots * count * block_width * vocab,
            bytes_accessed=2 * count * block_width * (vocab + slots),
            transcendentals=slots * vocab if closing else 0,
        ),
    )(index, *operands)


def finish_kernel(index_ref, doc_ref, all_ref, token_ref, score_ref):
    pack = index_ref[0]
    members = all_ref.shape[0]
    both = all_ref[...]

    def log_prob(at):
        logs = [both[i, at : at + 1, :] for i in range(members)]
        highest = functools.reduce(jnp.maximum, logs)
        summed = functools.reduce(jnp.add, [jnp.exp(one - highest) for one in logs])
        logit = functools.reduce(jnp.add, [both[i, at + 1 : at + 2, :] for i in range(members)])
        return logit - (highest + jnp.log(summed))

    ids = doc_ref[pl.ds(pack, 1), :]
    diff = jnp.where(ids >= 0, log_prob(2) - log_prob(0), 0.0)
    token_ref[...] = diff
    rows = ids.shape[1]
    number = lax.broadcasted_iota(jnp.int32, (DOC_PACK, rows), 0) + pack * DOC_PACK
    mine = number == ids
    sums = jnp.sum(jnp.where(mine, diff, 0.0), axis=1, keepdims=True)
    counts = jnp.sum(jnp.where(mine, 1.0, 0.0), axis=1, keepdims=True)
    score = sums / counts
    row = lax.broadcasted_iota(jnp.int32, (DOC_PACK, DOC_PACK), 0)
    column = lax.broadcasted_iota(jnp.int32, (DOC_PACK, DOC_PACK), 1)
    score_ref[...] = jnp.sum(jnp.where(row == column, score, 0.0), axis=0, keepdims=True)


def finish(gathered, doc, index):
    rows = doc.shape[1]
    token, score = pl.pallas_call(
        finish_kernel,
        out_shape=(
            jax.ShapeDtypeStruct((1, rows), jnp.float32),
            jax.ShapeDtypeStruct((1, DOC_PACK), jnp.float32),
        ),
        in_specs=[whole(SMEM), whole(), whole()],
        out_specs=(whole(), whole()),
    )(index, doc, gathered)
    return token.reshape(rows), score.reshape(DOC_PACK)


def per_device(gen_hidden, gen_gain, gen_head, dom_hidden, dom_gain, dom_head, targets, doc_ids):
    rows = gen_hidden.shape[0]
    gen_count = lax.axis_size("gen")
    dom_count = lax.axis_size("dom")
    gen_index = lax.axis_index("gen")
    dom_index = lax.axis_index("dom")
    first = (gen_index * dom_count + dom_index) * gen_head.shape[0]
    gen_at = jnp.stack([gen_index, first]).astype(jnp.int32)
    dom_at = jnp.stack([dom_index, first]).astype(jnp.int32)
    doc = doc_ids.reshape(dom_count, rows)
    target = targets.reshape(dom_count, rows)
    slots = dom_count // 2 * (rows + DOC_PACK)

    gen_first = around(gen_hidden, "dom")
    dom_first = around(dom_hidden, "gen")
    dom_rows, dom_square = compact(dom_first, doc, gen_at, slots)
    squares = around(dom_square, "dom")
    dom_parts = around(dom_rows, "dom")
    gen_rows, _ = compact(gen_first, doc, dom_at, slots)
    gen_parts = around(gen_rows, "gen")
    gen_numbers = [jnp.remainder(gen_index - k, gen_count) for k in range(gen_count)]
    dom_numbers = [jnp.remainder(dom_index - k, dom_count) for k in range(dom_count)]
    held = blocks(
        dom_parts[:1], dom_numbers[:1], first, squares, None, dom_gain, dom_head,
        doc, target, 1024, False,
    )
    gen_stats = blocks(
        gen_parts, gen_numbers, first, [], None, gen_gain, gen_head, doc, target,
        512, True,
    )
    dom_stats = blocks(
        dom_parts[1:], dom_numbers[1:], first, squares, held, dom_gain, dom_head,
        doc, target, 512, True,
    )
    both = jnp.concatenate([gen_stats, dom_stats], axis=1)
    sent = jnp.broadcast_to(both[None], (gen_count,) + both.shape)
    sent = sent.reshape((gen_count * dom_count,) + both.shape[1:])
    gathered = lax.all_to_all(sent, ("gen", "dom"), 0, 0)
    return finish(gathered, doc, dom_at)


def solution(mesh):
    in_specs = (
        P(("dp", "dom"), "gen"),
        P("dp"),
        P(("dp", "gen", "dom"), None),
        P(("dp", "gen"), "dom"),
        P("dp"),
        P(("dp", "gen", "dom"), None),
        P("dp"),
        P("dp"),
    )
    out_specs = (P(("dp", "dom")), P(("dp", "dom")))
    return jax.shard_map(
        per_device, mesh=mesh, in_specs=in_specs, out_specs=out_specs, check_vma=False
    )
```

```python
import functools

import jax
import jax.numpy as jnp
from jax import lax
from jax.experimental import pallas as pl
from jax.experimental.pallas import tpu as pltpu
from jax.sharding import PartitionSpec as P


DOC_PACK = 8
EPS = 1e-05
HALVES = 2
VMEM = pltpu.VMEM
SMEM = pltpu.SMEM


def whole(memory_space=VMEM):
    return pl.BlockSpec(memory_space=memory_space)


def origin(axis, index, k, count):
    if axis == "gen" and count & (count - 1) == 0:
        return index ^ k
    return (index - k + count) % count


def around(block, axis):
    count = lax.axis_size(axis)
    parts = [block]
    for k in range(1, count):
        pairs = [(origin(axis, i, k, count), i) for i in range(count)]
        parts.append(lax.ppermute(block, axis, pairs))
    return parts


def pack_extents(doc):
    live = jnp.where(doc >= 0, 1.0, 0.0)
    counts = jnp.sum(live, axis=1, keepdims=True)
    ahead = jnp.zeros((1, 1), jnp.float32)
    extents = []
    for p in range(doc.shape[0]):
        count = counts[p : p + 1, :]
        extents.append((count, ahead))
        ahead = ahead + count
    return extents


def slot_mask(extent, slots, rows):
    count, ahead = extent
    slot = lax.broadcasted_iota(jnp.int32, (slots, rows), 0).astype(jnp.float32)
    row = lax.broadcasted_iota(jnp.int32, (slots, rows), 1).astype(jnp.float32)
    return (slot - ahead == row) & (row < count)


def compact_kernel(pack_axis, spans, index_ref, doc_ref, *refs):
    part_refs = refs[:-2] if spans else refs[:-1]
    out_ref = refs[len(part_refs)]
    packs, rows = doc_ref.shape
    slots = out_ref.shape[0]
    extents = pack_extents(doc_ref[...])
    mine = index_ref[0]
    total = None
    for k, part_ref in enumerate(part_refs):
        pack = origin(pack_axis, mine, k, packs)
        count = jnp.zeros((1, 1), jnp.float32)
        ahead = jnp.zeros((1, 1), jnp.float32)
        for p in range(packs):
            here = jnp.where(pack == p, 1.0, 0.0)
            count = count + extents[p][0] * here
            ahead = ahead + extents[p][1] * here
        mask = slot_mask((count, ahead), slots, rows)
        onehot = jnp.where(mask, 1.0, 0.0).astype(jnp.bfloat16)
        piece = jnp.dot(onehot, part_ref[...], preferred_element_type=jnp.float32)
        total = piece if total is None else total + piece
    out_ref[...] = total.astype(jnp.bfloat16)
    if spans:
        span_ref = refs[-1]
        width = span_ref.shape[1]
        start = pl.multiple_of(lax.rem(mine, spans) * width, width)
        span_ref[...] = out_ref[:, pl.ds(start, width)]


def compact(parts, doc, index, slots, pack_axis, spans=0):
    width = parts[0].shape[1]
    out_shape = [jax.ShapeDtypeStruct((slots, width), jnp.bfloat16)]
    if spans:
        out_shape.append(jax.ShapeDtypeStruct((slots, width // spans), jnp.bfloat16))
    return pl.pallas_call(
        functools.partial(compact_kernel, pack_axis, spans),
        out_shape=out_shape,
        in_specs=[whole(SMEM), whole()] + [whole() for _ in parts],
        out_specs=[whole()] * len(out_shape),
        compiler_params=pltpu.CompilerParams(vmem_limit_bytes=16 * 1024 * 1024),
        cost_estimate=pl.CostEstimate(
            flops=2 * slots * width * doc.size,
            bytes_accessed=2 * width * (doc.size + slots),
            transcendentals=0,
        ),
    )(index, doc, *parts)


def tally(logits, wanted, top, total, picked):
    lanes = top.shape[1]
    groups = [logits[:, at : at + lanes] for at in range(0, logits.shape[1], lanes)]
    former = top[...]
    highest = functools.reduce(jnp.maximum, groups, former)
    lane = lax.broadcasted_iota(jnp.int32, former.shape, 1)
    away = wanted - lane
    latest = total[...] * jnp.exp(former - highest)
    hit = picked[...]
    for k, group in enumerate(groups):
        latest = latest + jnp.exp(group - highest)
        hit = jnp.where(away == k * lanes, group, hit)
    top[...] = highest
    total[...] = latest
    picked[...] = hit


def summed_up(top, total, picked):
    highest = jnp.max(top[...], axis=1, keepdims=True)
    everything = jnp.sum(total[...] * jnp.exp(top[...] - highest), axis=1, keepdims=True)
    return highest + jnp.log(everything), jnp.sum(picked[...], axis=1, keepdims=True)


def stats_kernel(pieces, buffers, index_ref, doc_ref, target_ref, gain_ref, head_ref, *refs):
    part_count = pieces[-1][0] + 1
    part_refs = refs[:part_count]
    out_ref, normed, tiles, sems, top, total, picked, wanted = refs[part_count:]
    slots, width = normed.shape
    tile = tiles.shape[1]
    packs, rows = doc_ref.shape
    j = pl.program_id(0)
    steps = pl.num_programs(0)

    def copy(step):
        slot = lax.rem(step, buffers)
        return pltpu.make_async_copy(
            head_ref.at[pl.ds(pl.multiple_of(step * tile, tile), tile), :],
            tiles.at[slot],
            sems.at[slot],
        )

    @pl.when(j == 0)
    def _():
        copy(0).start()
        for step in range(1, buffers - 1):
            pl.when(step < steps)(lambda: copy(step).start())

    @pl.when(j + buffers - 1 < steps)
    def _():
        copy(j + buffers - 1).start()

    @pl.when(j == 0)
    def _():
        sums = jnp.zeros((slots, 1), jnp.float32)
        for part_ref in part_refs:
            values = part_ref[...].astype(jnp.float32)
            sums = sums + jnp.sum(values * values, axis=1, keepdims=True)
        scale = lax.rsqrt(sums / width + EPS)
        for k, (part, start, extent) in enumerate(pieces):
            at = pl.ds(pl.multiple_of(index_ref[k], 128), extent)
            values = part_refs[part][:, start : start + extent].astype(jnp.float32)
            normed[:, at] = (values * scale * gain_ref[:, at]).astype(jnp.bfloat16)
        extents = pack_extents(doc_ref[...])
        ids = jnp.zeros((slots, 1), jnp.float32)
        for p in range(packs):
            mask = slot_mask(extents[p], slots, rows)
            row = (target_ref[p : p + 1, :] - index_ref[len(pieces)]).astype(jnp.float32)
            ids = ids + jnp.sum(jnp.where(mask, row, 0.0), axis=1, keepdims=True)
        wanted[...] = jnp.broadcast_to(ids.astype(jnp.int32), wanted.shape)
        top[...] = jnp.full(top.shape, -jnp.inf, jnp.float32)
        total[...] = jnp.zeros(total.shape, jnp.float32)
        picked[...] = jnp.zeros(picked.shape, jnp.float32)

    copy(j).wait()
    logits = lax.dot_general(
        normed[...],
        tiles[lax.rem(j, buffers)],
        (((1,), (1,)), ((), ())),
        preferred_element_type=jnp.float32,
    )
    tally(logits, wanted[...] - j * tile, top, total, picked)

    @pl.when(j == steps - 1)
    def _():
        log_total, logit = summed_up(top, total, picked)
        extents = pack_extents(doc_ref[...])
        for p in range(packs):
            mask = slot_mask(extents[p], slots, rows)
            out_ref[p, 0:1, :] = jnp.sum(jnp.where(mask, log_total, 0.0), axis=0, keepdims=True)
            out_ref[p, 1:2, :] = jnp.sum(jnp.where(mask, logit, 0.0), axis=0, keepdims=True)


def stats(parts, first, gain, head, doc, target):
    slots = parts[0][0].shape[0]
    vocab, width = head.shape
    packs, rows = doc.shape
    tile = min(512, vocab)
    buffers = 3
    pieces, starts = [], []
    for number, (array, places) in enumerate(parts):
        extent = array.shape[1] // len(places)
        for k, place in enumerate(places):
            pieces.append((number, k * extent, extent))
            starts.append(place)
    index = jnp.stack(starts + [first]).astype(jnp.int32)
    column = VMEM((slots, 128), jnp.float32)
    return pl.pallas_call(
        functools.partial(stats_kernel, tuple(pieces), buffers),
        grid=(vocab // tile,),
        in_specs=[whole(SMEM), whole(), whole(), whole(), whole(pl.ANY)] + [whole() for _ in parts],
        out_specs=whole(),
        out_shape=jax.ShapeDtypeStruct((packs, 2, rows), jnp.float32),
        scratch_shapes=[
            VMEM((slots, width), jnp.bfloat16),
            VMEM((buffers, tile, width), jnp.bfloat16),
            pltpu.SemaphoreType.DMA((buffers,)),
            column,
            column,
            column,
            VMEM((slots, 128), jnp.int32),
        ],
        compiler_params=pltpu.CompilerParams(vmem_limit_bytes=32 * 1024 * 1024),
        cost_estimate=pl.CostEstimate(
            flops=2 * slots * width * vocab,
            bytes_accessed=2 * width * (vocab + slots),
            transcendentals=slots * vocab,
        ),
    )(index, doc, target, gain.reshape(1, width), head, *[array for array, _ in parts])


def finish_kernel(index_ref, doc_ref, all_ref, token_ref, score_ref):
    pack = index_ref[0]
    members = all_ref.shape[0]
    both = all_ref[...]

    def log_prob(at):
        logs = [both[i, at : at + 1, :] for i in range(members)]
        highest = functools.reduce(jnp.maximum, logs)
        summed = functools.reduce(jnp.add, [jnp.exp(one - highest) for one in logs])
        logit = functools.reduce(jnp.add, [both[i, at + 1 : at + 2, :] for i in range(members)])
        return logit - (highest + jnp.log(summed))

    ids = doc_ref[pl.ds(pack, 1), :]
    diff = jnp.where(ids >= 0, log_prob(2) - log_prob(0), 0.0)
    token_ref[...] = diff
    rows = ids.shape[1]
    number = lax.broadcasted_iota(jnp.int32, (DOC_PACK, rows), 0) + pack * DOC_PACK
    mine = number == ids
    sums = jnp.sum(jnp.where(mine, diff, 0.0), axis=1, keepdims=True)
    counts = jnp.sum(jnp.where(mine, 1.0, 0.0), axis=1, keepdims=True)
    score = sums / counts
    row = lax.broadcasted_iota(jnp.int32, (DOC_PACK, DOC_PACK), 0)
    column = lax.broadcasted_iota(jnp.int32, (DOC_PACK, DOC_PACK), 1)
    score_ref[...] = jnp.sum(jnp.where(row == column, score, 0.0), axis=0, keepdims=True)


def finish(gathered, doc, index):
    rows = doc.shape[1]
    token, score = pl.pallas_call(
        finish_kernel,
        out_shape=(
            jax.ShapeDtypeStruct((1, rows), jnp.float32),
            jax.ShapeDtypeStruct((1, DOC_PACK), jnp.float32),
        ),
        in_specs=[whole(SMEM), whole(), whole()],
        out_specs=(whole(), whole()),
    )(index, doc, gathered)
    return token.reshape(rows), score.reshape(DOC_PACK)


def per_device(gen_hidden, gen_gain, gen_head, dom_hidden, dom_gain, dom_head, targets, doc_ids):
    rows = gen_hidden.shape[0]
    gen_count = lax.axis_size("gen")
    dom_count = lax.axis_size("dom")
    gen_index = lax.axis_index("gen")
    dom_index = lax.axis_index("dom")
    first = (gen_index * dom_count + dom_index) * gen_head.shape[0]
    gen_at = jnp.stack([gen_index, first]).astype(jnp.int32)
    dom_at = jnp.stack([dom_index, first]).astype(jnp.int32)
    doc = doc_ids.reshape(dom_count, rows)
    target = targets.reshape(dom_count, rows)
    slots = dom_count // 2 * (rows + DOC_PACK)

    block_width = gen_hidden.shape[1]
    half = block_width // HALVES
    dom_width = dom_hidden.shape[1]
    spans = gen_count if dom_width % (gen_count * 128) == 0 else 0
    gen_first = [around(gen_hidden[:, h * half : (h + 1) * half], "dom") for h in range(HALVES)]
    dom_first = around(dom_hidden, "gen")
    gen_parts = []
    for h in range(HALVES):
        (rows_in,) = compact(gen_first[h], doc, dom_at, slots, "dom")
        for k, part in enumerate(around(rows_in, "gen")):
            place = origin("gen", gen_index, k, gen_count) * block_width + h * half
            gen_parts.append((part, [place]))
    dom_rows, *dom_span = compact(dom_first, doc, gen_at, slots, "gen", spans)
    places = [origin("dom", dom_index, k, dom_count) * dom_width for k in range(dom_count)]
    dom_parts = [(dom_rows, places[:1])]
    if spans:
        span = dom_width // spans
        received = around(dom_span[0], "dom")[1:]
        joined = jnp.concatenate(received, axis=1)
        for k, part in enumerate(around(joined, "gen")):
            at = origin("gen", gen_index, k, gen_count) * span
            dom_parts.append((part, [place + at for place in places[1:]]))
    else:
        for k, part in enumerate(around(dom_rows, "dom")[1:]):
            dom_parts.append((part, places[k + 1 : k + 2]))
    gen_stats = stats(gen_parts, first, gen_gain, gen_head, doc, target)
    dom_stats = stats(dom_parts, first, dom_gain, dom_head, doc, target)
    both = jnp.concatenate([gen_stats, dom_stats], axis=1)
    sent = jnp.broadcast_to(both[None], (gen_count,) + both.shape)
    sent = sent.reshape((gen_count * dom_count,) + both.shape[1:])
    gathered = lax.all_to_all(sent, ("gen", "dom"), 0, 0)
    return finish(gathered, doc, dom_at)


def solution(mesh):
    in_specs = (
        P(("dp", "dom"), "gen"),
        P("dp"),
        P(("dp", "gen", "dom"), None),
        P(("dp", "gen"), "dom"),
        P("dp"),
        P(("dp", "gen", "dom"), None),
        P("dp"),
        P("dp"),
    )
    out_specs = (P(("dp", "dom")), P(("dp", "dom")))
    return jax.shard_map(
        per_device, mesh=mesh, in_specs=in_specs, out_specs=out_specs, check_vma=False
    )
```

```python
import functools

import jax
import jax.numpy as jnp
from jax import lax
from jax.experimental import pallas as pl
from jax.experimental.pallas import tpu as pltpu
from jax.sharding import PartitionSpec as P


DOC_PACK = 8
EPS = 1e-05
PORTIONS = (3, 5)
VMEM = pltpu.VMEM


def whole(memory_space=VMEM):
    return pl.BlockSpec(memory_space=memory_space)


def origin(axis, index, k, count):
    if axis == "gen" and count & (count - 1) == 0:
        return index ^ k
    return (index - k + count) % count


def portions(width):
    edges, done = [0], 0
    for portion in PORTIONS[:-1]:
        done += portion
        edge = max(width * done // sum(PORTIONS) // 128 * 128, edges[-1] + 128)
        edges.append(edge)
    edges.append(width)
    return list(zip(edges, edges[1:]))


def around(block, axis):
    count = lax.axis_size(axis)
    parts = [block]
    for k in range(1, count):
        pairs = [(origin(axis, i, k, count), i) for i in range(count)]
        parts.append(lax.ppermute(block, axis, pairs))
    return parts


def pack_extents(doc):
    live = jnp.where(doc >= 0, 1.0, 0.0)
    counts = jnp.sum(live, axis=1, keepdims=True)
    ahead = jnp.zeros((1, 1), jnp.float32)
    extents = []
    for p in range(doc.shape[0]):
        count = counts[p : p + 1, :]
        extents.append((count, ahead))
        ahead = ahead + count
    return extents


def slot_mask(extent, slots, rows):
    count, ahead = extent
    slot = lax.broadcasted_iota(jnp.int32, (slots, rows), 0).astype(jnp.float32)
    row = lax.broadcasted_iota(jnp.int32, (slots, rows), 1).astype(jnp.float32)
    return (slot - ahead == row) & (row < count)


def prepare_kernel(vocab, *refs):
    doc_ref, target_ref, gen_gain_ref, dom_gain_ref, rows_ref = refs[:5]
    doc_out, live_ref, wanted_ref, gen_gain_out, dom_gain_out, rows_out = refs[5:]
    doc_out[...] = doc_ref[...]
    gen_gain_out[...] = gen_gain_ref[...]
    dom_gain_out[...] = dom_gain_ref[...]
    rows_out[...] = rows_ref[...]
    packs, rows = doc_ref.shape
    slots = live_ref.shape[0]
    extents = pack_extents(doc_ref[...])
    device = lax.axis_index("gen") * lax.axis_size("dom") + lax.axis_index("dom")
    ids = jnp.zeros((slots, 1), jnp.float32)
    for p in range(packs):
        mask = slot_mask(extents[p], slots, rows)
        live_ref[:, p * rows : (p + 1) * rows] = jnp.where(mask, 1.0, 0.0).astype(jnp.bfloat16)
        row = (target_ref[p : p + 1, :] - device * vocab).astype(jnp.float32)
        ids = ids + jnp.sum(jnp.where(mask, row, 0.0), axis=1, keepdims=True)
    wanted_ref[...] = jnp.broadcast_to(ids.astype(jnp.int32), wanted_ref.shape)


def prepare(doc, target, gen_gain, dom_gain, rows_in, slots, vocab):
    like = lambda x: jax.ShapeDtypeStruct(x.shape, x.dtype)
    return pl.pallas_call(
        functools.partial(prepare_kernel, vocab),
        out_shape=(
            like(doc),
            jax.ShapeDtypeStruct((slots, doc.size), jnp.bfloat16),
            jax.ShapeDtypeStruct((slots, 128), jnp.int32),
            like(gen_gain),
            like(dom_gain),
            like(rows_in),
        ),
        in_specs=[whole()] * 5,
        out_specs=[whole()] * 6,
        compiler_params=pltpu.CompilerParams(vmem_limit_bytes=8 * 1024 * 1024),
    )(doc, target, gen_gain, dom_gain, rows_in)


def compact_kernel(pack_axis, spans, live_ref, *refs):
    part_refs = refs[:-2] if spans else refs[:-1]
    out_ref = refs[len(part_refs)]
    rows = part_refs[0].shape[0]
    mine = lax.axis_index(pack_axis)
    total = None
    for k, part_ref in enumerate(part_refs):
        pack = origin(pack_axis, mine, k, len(part_refs))
        live = live_ref[:, pl.ds(pl.multiple_of(pack * rows, rows), rows)]
        piece = jnp.dot(live, part_ref[...], preferred_element_type=jnp.float32)
        total = piece if total is None else total + piece
    out_ref[...] = total.astype(jnp.bfloat16)
    if spans:
        span_ref = refs[-1]
        width = span_ref.shape[1]
        start = pl.multiple_of(mine * width, width)
        span_ref[...] = out_ref[:, pl.ds(start, width)]


def compact(parts, live, pack_axis, spans=0):
    width = parts[0].shape[1]
    slots = live.shape[0]
    out_shape = [jax.ShapeDtypeStruct((slots, width), jnp.bfloat16)]
    if spans:
        out_shape.append(jax.ShapeDtypeStruct((slots, width // spans), jnp.bfloat16))
    return pl.pallas_call(
        functools.partial(compact_kernel, pack_axis, spans),
        out_shape=out_shape,
        in_specs=[whole()] * (1 + len(parts)),
        out_specs=[whole()] * len(out_shape),
        compiler_params=pltpu.CompilerParams(vmem_limit_bytes=16 * 1024 * 1024),
        cost_estimate=pl.CostEstimate(
            flops=2 * width * live.size,
            bytes_accessed=2 * width * (live.shape[1] + slots),
            transcendentals=0,
        ),
    )(live, *parts)


def tally(logits, wanted, top, total, picked):
    lanes = top.shape[1]
    groups = [logits[:, at : at + lanes] for at in range(0, logits.shape[1], lanes)]
    former = top[...]
    highest = functools.reduce(jnp.maximum, groups, former)
    lane = lax.broadcasted_iota(jnp.int32, former.shape, 1)
    away = wanted - lane
    latest = total[...] * jnp.exp(former - highest)
    hit = picked[...]
    for k, group in enumerate(groups):
        latest = latest + jnp.exp(group - highest)
        hit = jnp.where(away == k * lanes, group, hit)
    top[...] = highest
    total[...] = latest
    picked[...] = hit


def summed_up(top, total, picked):
    highest = jnp.max(top[...], axis=1, keepdims=True)
    everything = jnp.sum(total[...] * jnp.exp(top[...] - highest), axis=1, keepdims=True)
    return highest + jnp.log(everything), jnp.sum(picked[...], axis=1, keepdims=True)


def stats_kernel(pieces, buffers, wanted_ref, live_ref, gain_ref, head_ref, *refs):
    part_count = pieces[-1][0] + 1
    part_refs = refs[:part_count]
    out_ref, normed, tiles, sems, top, total, picked = refs[part_count:]
    slots, width = normed.shape
    tile = tiles.shape[1]
    packs, _, rows = out_ref.shape
    j = pl.program_id(0)
    steps = pl.num_programs(0)

    def copy(step):
        slot = lax.rem(step, buffers)
        return pltpu.make_async_copy(
            head_ref.at[pl.ds(pl.multiple_of(step * tile, tile), tile), :],
            tiles.at[slot],
            sems.at[slot],
        )

    @pl.when(j == 0)
    def _():
        copy(0).start()
        for step in range(1, buffers - 1):
            pl.when(step < steps)(lambda: copy(step).start())

    @pl.when(j + buffers - 1 < steps)
    def _():
        copy(j + buffers - 1).start()

    @pl.when(j == 0)
    def _():
        sums = jnp.zeros((slots, 1), jnp.float32)
        for part_ref in part_refs:
            values = part_ref[...].astype(jnp.float32)
            sums = sums + jnp.sum(values * values, axis=1, keepdims=True)
        scale = lax.rsqrt(sums / width + EPS)
        for part, start, extent, place in pieces:
            at = pl.ds(pl.multiple_of(place(), 128), extent)
            values = part_refs[part][:, start : start + extent].astype(jnp.float32)
            normed[:, at] = (values * scale * gain_ref[:, at]).astype(jnp.bfloat16)
        top[...] = jnp.full(top.shape, -jnp.inf, jnp.float32)
        total[...] = jnp.zeros(total.shape, jnp.float32)
        picked[...] = jnp.zeros(picked.shape, jnp.float32)

    copy(j).wait()
    logits = lax.dot_general(
        normed[...],
        tiles[lax.rem(j, buffers)],
        (((1,), (1,)), ((), ())),
        preferred_element_type=jnp.float32,
    )
    tally(logits, wanted_ref[...] - j * tile, top, total, picked)

    @pl.when(j == steps - 1)
    def _():
        log_total, logit = summed_up(top, total, picked)
        for p in range(packs):
            mask = live_ref[:, p * rows : (p + 1) * rows].astype(jnp.float32) > 0.5
            out_ref[p, 0:1, :] = jnp.sum(jnp.where(mask, log_total, 0.0), axis=0, keepdims=True)
            out_ref[p, 1:2, :] = jnp.sum(jnp.where(mask, logit, 0.0), axis=0, keepdims=True)


def stats(parts, gain, head, wanted, live, packs):
    slots = parts[0][0].shape[0]
    vocab, width = head.shape
    rows = live.shape[1] // packs
    tile = min(512, vocab)
    buffers = 3
    pieces = []
    for number, (array, places) in enumerate(parts):
        extent = array.shape[1] // len(places)
        for k, place in enumerate(places):
            pieces.append((number, k * extent, extent, place))
    column = VMEM((slots, 128), jnp.float32)
    return pl.pallas_call(
        functools.partial(stats_kernel, tuple(pieces), buffers),
        grid=(vocab // tile,),
        in_specs=[whole(), whole(), whole(), whole(pl.ANY)] + [whole() for _ in parts],
        out_specs=whole(),
        out_shape=jax.ShapeDtypeStruct((packs, 2, rows), jnp.float32),
        scratch_shapes=[
            VMEM((slots, width), jnp.bfloat16),
            VMEM((buffers, tile, width), jnp.bfloat16),
            pltpu.SemaphoreType.DMA((buffers,)),
            column,
            column,
            column,
        ],
        compiler_params=pltpu.CompilerParams(vmem_limit_bytes=32 * 1024 * 1024),
        cost_estimate=pl.CostEstimate(
            flops=2 * slots * width * vocab,
            bytes_accessed=2 * width * (vocab + slots),
            transcendentals=slots * vocab,
        ),
    )(wanted, live, gain, head, *[array for array, _ in parts])


def finish_kernel(doc_ref, all_ref, token_ref, score_ref):
    pack = lax.axis_index("dom")
    members = all_ref.shape[0]
    both = all_ref[...]

    def log_prob(at):
        logs = [both[i, at : at + 1, :] for i in range(members)]
        highest = functools.reduce(jnp.maximum, logs)
        summed = functools.reduce(jnp.add, [jnp.exp(one - highest) for one in logs])
        logit = functools.reduce(jnp.add, [both[i, at + 1 : at + 2, :] for i in range(members)])
        return logit - (highest + jnp.log(summed))

    ids = doc_ref[pl.ds(pack, 1), :]
    diff = jnp.where(ids >= 0, log_prob(2) - log_prob(0), 0.0)
    token_ref[...] = diff
    rows = ids.shape[1]
    number = lax.broadcasted_iota(jnp.int32, (DOC_PACK, rows), 0) + pack * DOC_PACK
    mine = number == ids
    sums = jnp.sum(jnp.where(mine, diff, 0.0), axis=1, keepdims=True)
    counts = jnp.sum(jnp.where(mine, 1.0, 0.0), axis=1, keepdims=True)
    score = sums / counts
    row = lax.broadcasted_iota(jnp.int32, (DOC_PACK, DOC_PACK), 0)
    column = lax.broadcasted_iota(jnp.int32, (DOC_PACK, DOC_PACK), 1)
    score_ref[...] = jnp.sum(jnp.where(row == column, score, 0.0), axis=0, keepdims=True)


def finish(gathered, doc):
    rows = doc.shape[1]
    token, score = pl.pallas_call(
        finish_kernel,
        out_shape=(
            jax.ShapeDtypeStruct((1, rows), jnp.float32),
            jax.ShapeDtypeStruct((1, DOC_PACK), jnp.float32),
        ),
        in_specs=[whole(), whole()],
        out_specs=(whole(), whole()),
        compiler_params=pltpu.CompilerParams(vmem_limit_bytes=8 * 1024 * 1024),
    )(doc, gathered)
    return token.reshape(rows), score.reshape(DOC_PACK)


def per_device(gen_hidden, gen_gain, gen_head, dom_hidden, dom_gain, dom_head, targets, doc_ids):
    rows = gen_hidden.shape[0]
    gen_count = lax.axis_size("gen")
    dom_count = lax.axis_size("dom")
    doc = doc_ids.reshape(dom_count, rows)
    target = targets.reshape(dom_count, rows)
    slots = dom_count // 2 * (rows + DOC_PACK)
    width = gen_head.shape[1]
    block_width = gen_hidden.shape[1]
    cuts = portions(block_width)
    dom_width = dom_hidden.shape[1]
    spans = gen_count if dom_width % (gen_count * 128) == 0 else 0
    gen_from = lambda k: origin("gen", lax.axis_index("gen"), k, gen_count)
    dom_from = lambda k: origin("dom", lax.axis_index("dom"), k, dom_count)
    doc, live, wanted, gen_gain, dom_gain, dom_own = prepare(
        doc, target, gen_gain.reshape(1, width), dom_gain.reshape(1, width), dom_hidden,
        slots, gen_head.shape[0],
    )
    gen_first = [around(gen_hidden[:, start:stop], "dom") for start, stop in cuts]
    dom_first = around(dom_hidden, "gen")
    gen_parts = []
    for h, (start, _) in enumerate(cuts):
        (rows_in,) = compact(gen_first[h], live, "dom")
        for k, part in enumerate(around(rows_in, "gen")):
            place = lambda k=k, start=start: gen_from(k) * block_width + start
            gen_parts.append((part, [place]))
    dom_rows, *dom_span = compact([dom_own] + dom_first[1:], live, "gen", spans)
    dom_parts = [(dom_rows, [lambda: dom_from(0) * dom_width])]
    if spans:
        span = dom_width // spans
        received = around(dom_span[0], "dom")[1:]
        joined = jnp.concatenate(received, axis=1)
        for k, part in enumerate(around(joined, "gen")):
            places = [
                lambda k=k, i=i: dom_from(i) * dom_width + gen_from(k) * span
                for i in range(1, dom_count)
            ]
            dom_parts.append((part, places))
    else:
        for k, part in enumerate(around(dom_rows, "dom")[1:]):
            dom_parts.append((part, [lambda k=k: dom_from(k + 1) * dom_width]))
    gen_stats = stats(gen_parts, gen_gain, gen_head, wanted, live, dom_count)
    dom_stats = stats(dom_parts, dom_gain, dom_head, wanted, live, dom_count)
    both = jnp.concatenate([gen_stats, dom_stats], axis=1)
    sent = jnp.broadcast_to(both[None], (gen_count,) + both.shape)
    sent = sent.reshape((gen_count * dom_count,) + both.shape[1:])
    gathered = lax.all_to_all(sent, ("gen", "dom"), 0, 0)
    return finish(gathered, doc)


def solution(mesh):
    in_specs = (
        P(("dp", "dom"), "gen"),
        P("dp"),
        P(("dp", "gen", "dom"), None),
        P(("dp", "gen"), "dom"),
        P("dp"),
        P(("dp", "gen", "dom"), None),
        P("dp"),
        P("dp"),
    )
    out_specs = (P(("dp", "dom")), P(("dp", "dom")))
    return jax.shard_map(
        per_device, mesh=mesh, in_specs=in_specs, out_specs=out_specs, check_vma=False
    )
```

```python
import functools

import jax
import jax.numpy as jnp
from jax import lax
from jax.experimental import pallas as pl
from jax.experimental.pallas import tpu as pltpu
from jax.sharding import PartitionSpec as P


DOC_PACK = 8
EPS = 1e-05
PORTIONS = (3, 5)
VMEM = pltpu.VMEM


def whole(memory_space=VMEM):
    return pl.BlockSpec(memory_space=memory_space)


def origin(axis, index, k, count):
    if axis == "gen" and count & (count - 1) == 0:
        return index ^ k
    return (index - k + count) % count


def portions(width):
    edges, done = [0], 0
    for portion in PORTIONS[:-1]:
        done += portion
        edge = max(width * done // sum(PORTIONS) // 128 * 128, edges[-1] + 128)
        edges.append(edge)
    edges.append(width)
    return list(zip(edges, edges[1:]))


def moved(block, axis, k):
    count = lax.axis_size(axis)
    pairs = [(origin(axis, i, k, count), i) for i in range(count)]
    return lax.ppermute(block, axis, pairs)


def around(block, axis):
    return [block] + [moved(block, axis, k) for k in range(1, lax.axis_size(axis))]


def pack_extents(doc):
    live = jnp.where(doc >= 0, 1.0, 0.0)
    counts = jnp.sum(live, axis=1, keepdims=True)
    ahead = jnp.zeros((1, 1), jnp.float32)
    extents = []
    for p in range(doc.shape[0]):
        count = counts[p : p + 1, :]
        extents.append((count, ahead))
        ahead = ahead + count
    return extents


def slot_mask(extent, slots, rows):
    count, ahead = extent
    slot = lax.broadcasted_iota(jnp.int32, (slots, rows), 0).astype(jnp.float32)
    row = lax.broadcasted_iota(jnp.int32, (slots, rows), 1).astype(jnp.float32)
    return (slot - ahead == row) & (row < count)


def prepare_kernel(vocab, *refs):
    doc_ref, target_ref, gen_gain_ref, dom_gain_ref, rows_ref = refs[:5]
    doc_out, live_ref, wanted_ref, gen_gain_out, dom_gain_out, rows_out = refs[5:]
    doc_out[...] = doc_ref[...]
    gen_gain_out[...] = gen_gain_ref[...]
    dom_gain_out[...] = dom_gain_ref[...]
    rows_out[...] = rows_ref[...]
    packs, rows = doc_ref.shape
    slots = live_ref.shape[0]
    extents = pack_extents(doc_ref[...])
    device = lax.axis_index("gen") * lax.axis_size("dom") + lax.axis_index("dom")
    ids = jnp.zeros((slots, 1), jnp.float32)
    for p in range(packs):
        mask = slot_mask(extents[p], slots, rows)
        live_ref[:, p * rows : (p + 1) * rows] = jnp.where(mask, 1.0, 0.0).astype(jnp.bfloat16)
        row = (target_ref[p : p + 1, :] - device * vocab).astype(jnp.float32)
        ids = ids + jnp.sum(jnp.where(mask, row, 0.0), axis=1, keepdims=True)
    wanted_ref[...] = jnp.broadcast_to(ids.astype(jnp.int32), wanted_ref.shape)


def prepare(doc, target, gen_gain, dom_gain, rows_in, slots, vocab):
    like = lambda x: jax.ShapeDtypeStruct(x.shape, x.dtype)
    return pl.pallas_call(
        functools.partial(prepare_kernel, vocab),
        out_shape=(
            like(doc),
            jax.ShapeDtypeStruct((slots, doc.size), jnp.bfloat16),
            jax.ShapeDtypeStruct((slots, 128), jnp.int32),
            like(gen_gain),
            like(dom_gain),
            like(rows_in),
        ),
        in_specs=[whole()] * 5,
        out_specs=[whole()] * 6,
        compiler_params=pltpu.CompilerParams(vmem_limit_bytes=8 * 1024 * 1024),
    )(doc, target, gen_gain, dom_gain, rows_in)


def compact_kernel(pack_axis, spans, live_ref, *refs):
    part_refs = refs[:-2] if spans else refs[:-1]
    out_ref = refs[len(part_refs)]
    rows = part_refs[0].shape[0]
    mine = lax.axis_index(pack_axis)
    total = None
    for k, part_ref in enumerate(part_refs):
        pack = origin(pack_axis, mine, k, len(part_refs))
        live = live_ref[:, pl.ds(pl.multiple_of(pack * rows, rows), rows)]
        piece = jnp.dot(live, part_ref[...], preferred_element_type=jnp.float32)
        total = piece if total is None else total + piece
    out_ref[...] = total.astype(jnp.bfloat16)
    if spans:
        span_ref = refs[-1]
        width = span_ref.shape[1]
        start = pl.multiple_of(mine * width, width)
        span_ref[...] = out_ref[:, pl.ds(start, width)]


def compact(parts, live, pack_axis, spans=0):
    width = parts[0].shape[1]
    slots = live.shape[0]
    out_shape = [jax.ShapeDtypeStruct((slots, width), jnp.bfloat16)]
    if spans:
        out_shape.append(jax.ShapeDtypeStruct((slots, width // spans), jnp.bfloat16))
    return pl.pallas_call(
        functools.partial(compact_kernel, pack_axis, spans),
        out_shape=out_shape,
        in_specs=[whole()] * (1 + len(parts)),
        out_specs=[whole()] * len(out_shape),
        compiler_params=pltpu.CompilerParams(vmem_limit_bytes=16 * 1024 * 1024),
        cost_estimate=pl.CostEstimate(
            flops=2 * width * live.size,
            bytes_accessed=2 * width * (live.shape[1] + slots),
            transcendentals=0,
        ),
    )(live, *parts)


def tally(logits, wanted, top, total, picked):
    lanes = top.shape[1]
    groups = [logits[:, at : at + lanes] for at in range(0, logits.shape[1], lanes)]
    former = top[...]
    highest = functools.reduce(jnp.maximum, groups, former)
    lane = lax.broadcasted_iota(jnp.int32, former.shape, 1)
    away = wanted - lane
    latest = total[...] * jnp.exp(former - highest)
    hit = picked[...]
    for k, group in enumerate(groups):
        latest = latest + jnp.exp(group - highest)
        hit = jnp.where(away == k * lanes, group, hit)
    top[...] = highest
    total[...] = latest
    picked[...] = hit


def summed_up(top, total, picked):
    highest = jnp.max(top[...], axis=1, keepdims=True)
    everything = jnp.sum(total[...] * jnp.exp(top[...] - highest), axis=1, keepdims=True)
    return highest + jnp.log(everything), jnp.sum(picked[...], axis=1, keepdims=True)


def stats_kernel(pieces, buffers, wanted_ref, live_ref, gain_ref, head_ref, *refs):
    part_count = pieces[-1][0] + 1
    part_refs = refs[:part_count]
    out_ref, normed, tiles, sems, top, total, picked = refs[part_count:]
    slots, width = normed.shape
    tile = tiles.shape[1]
    packs, _, rows = out_ref.shape
    j = pl.program_id(0)
    steps = pl.num_programs(0)

    def copy(step):
        slot = lax.rem(step, buffers)
        return pltpu.make_async_copy(
            head_ref.at[pl.ds(pl.multiple_of(step * tile, tile), tile), :],
            tiles.at[slot],
            sems.at[slot],
        )

    @pl.when(j == 0)
    def _():
        copy(0).start()
        for step in range(1, buffers - 1):
            pl.when(step < steps)(lambda: copy(step).start())

    @pl.when(j + buffers - 1 < steps)
    def _():
        copy(j + buffers - 1).start()

    @pl.when(j == 0)
    def _():
        sums = jnp.zeros((slots, 1), jnp.float32)
        for part_ref in part_refs:
            values = part_ref[...].astype(jnp.float32)
            sums = sums + jnp.sum(values * values, axis=1, keepdims=True)
        scale = lax.rsqrt(sums / width + EPS)
        for part, start, extent, place in pieces:
            at = pl.ds(pl.multiple_of(place(), 128), extent)
            values = part_refs[part][:, start : start + extent].astype(jnp.float32)
            normed[:, at] = (values * scale * gain_ref[:, at]).astype(jnp.bfloat16)
        top[...] = jnp.full(top.shape, -jnp.inf, jnp.float32)
        total[...] = jnp.zeros(total.shape, jnp.float32)
        picked[...] = jnp.zeros(picked.shape, jnp.float32)

    copy(j).wait()
    logits = lax.dot_general(
        normed[...],
        tiles[lax.rem(j, buffers)],
        (((1,), (1,)), ((), ())),
        preferred_element_type=jnp.float32,
    )
    tally(logits, wanted_ref[...] - j * tile, top, total, picked)

    @pl.when(j == steps - 1)
    def _():
        log_total, logit = summed_up(top, total, picked)
        for p in range(packs):
            mask = live_ref[:, p * rows : (p + 1) * rows].astype(jnp.float32) > 0.5
            out_ref[p, 0:1, :] = jnp.sum(jnp.where(mask, log_total, 0.0), axis=0, keepdims=True)
            out_ref[p, 1:2, :] = jnp.sum(jnp.where(mask, logit, 0.0), axis=0, keepdims=True)


def stats(parts, gain, head, wanted, live, packs):
    slots = parts[0][0].shape[0]
    vocab, width = head.shape
    rows = live.shape[1] // packs
    tile = min(512, vocab)
    buffers = 3
    pieces = []
    for number, (array, places) in enumerate(parts):
        extent = array.shape[1] // len(places)
        for k, place in enumerate(places):
            pieces.append((number, k * extent, extent, place))
    column = VMEM((slots, 128), jnp.float32)
    return pl.pallas_call(
        functools.partial(stats_kernel, tuple(pieces), buffers),
        grid=(vocab // tile,),
        in_specs=[whole(), whole(), whole(), whole(pl.ANY)] + [whole() for _ in parts],
        out_specs=whole(),
        out_shape=jax.ShapeDtypeStruct((packs, 2, rows), jnp.float32),
        scratch_shapes=[
            VMEM((slots, width), jnp.bfloat16),
            VMEM((buffers, tile, width), jnp.bfloat16),
            pltpu.SemaphoreType.DMA((buffers,)),
            column,
            column,
            column,
        ],
        compiler_params=pltpu.CompilerParams(vmem_limit_bytes=32 * 1024 * 1024),
        cost_estimate=pl.CostEstimate(
            flops=2 * slots * width * vocab,
            bytes_accessed=2 * width * (vocab + slots),
            transcendentals=slots * vocab,
        ),
    )(wanted, live, gain, head, *[array for array, _ in parts])


def finish_kernel(doc_ref, all_ref, token_ref, score_ref):
    pack = lax.axis_index("dom")
    members = all_ref.shape[0]
    both = all_ref[...]

    def log_prob(at):
        logs = [both[i, at : at + 1, :] for i in range(members)]
        highest = functools.reduce(jnp.maximum, logs)
        summed = functools.reduce(jnp.add, [jnp.exp(one - highest) for one in logs])
        logit = functools.reduce(jnp.add, [both[i, at + 1 : at + 2, :] for i in range(members)])
        return logit - (highest + jnp.log(summed))

    ids = doc_ref[pl.ds(pack, 1), :]
    diff = jnp.where(ids >= 0, log_prob(2) - log_prob(0), 0.0)
    token_ref[...] = diff
    rows = ids.shape[1]
    number = lax.broadcasted_iota(jnp.int32, (DOC_PACK, rows), 0) + pack * DOC_PACK
    mine = number == ids
    sums = jnp.sum(jnp.where(mine, diff, 0.0), axis=1, keepdims=True)
    counts = jnp.sum(jnp.where(mine, 1.0, 0.0), axis=1, keepdims=True)
    score = sums / counts
    row = lax.broadcasted_iota(jnp.int32, (DOC_PACK, DOC_PACK), 0)
    column = lax.broadcasted_iota(jnp.int32, (DOC_PACK, DOC_PACK), 1)
    score_ref[...] = jnp.sum(jnp.where(row == column, score, 0.0), axis=0, keepdims=True)


def finish(gathered, doc):
    rows = doc.shape[1]
    token, score = pl.pallas_call(
        finish_kernel,
        out_shape=(
            jax.ShapeDtypeStruct((1, rows), jnp.float32),
            jax.ShapeDtypeStruct((1, DOC_PACK), jnp.float32),
        ),
        in_specs=[whole(), whole()],
        out_specs=(whole(), whole()),
        compiler_params=pltpu.CompilerParams(vmem_limit_bytes=8 * 1024 * 1024),
    )(doc, gathered)
    return token.reshape(rows), score.reshape(DOC_PACK)


def per_device(gen_hidden, gen_gain, gen_head, dom_hidden, dom_gain, dom_head, targets, doc_ids):
    rows = gen_hidden.shape[0]
    gen_count = lax.axis_size("gen")
    dom_count = lax.axis_size("dom")
    doc = doc_ids.reshape(dom_count, rows)
    target = targets.reshape(dom_count, rows)
    slots = dom_count // 2 * (rows + DOC_PACK)
    width = gen_head.shape[1]
    block_width = gen_hidden.shape[1]
    cuts = portions(block_width)
    dom_width = dom_hidden.shape[1]
    spans = gen_count if dom_width % (gen_count * 128) == 0 else 0
    gen_from = lambda k: origin("gen", lax.axis_index("gen"), k, gen_count)
    dom_from = lambda k: origin("dom", lax.axis_index("dom"), k, dom_count)
    doc, live, wanted, gen_gain, dom_gain, dom_own = prepare(
        doc, target, gen_gain.reshape(1, width), dom_gain.reshape(1, width), dom_hidden,
        slots, gen_head.shape[0],
    )
    gen_first = [around(gen_hidden[:, start:stop], "dom") for start, stop in cuts]
    dom_first = around(dom_hidden, "gen")
    gen_parts = []
    for h, (start, _) in enumerate(cuts):
        (rows_in,) = compact(gen_first[h], live, "dom")
        for k, part in enumerate(around(rows_in, "gen")):
            place = lambda k=k, start=start: gen_from(k) * block_width + start
            gen_parts.append((part, [place]))
    dom_rows, *dom_span = compact([dom_own] + dom_first[1:], live, "gen", spans)
    dom_parts = [(dom_rows, [lambda: dom_from(0) * dom_width])]
    if spans:
        span = dom_width // spans
        received = [moved(dom_span[0], "dom", k) for k in range(2, dom_count)]
        near = moved(dom_rows, "dom", 1)
        dom_parts.append((near, [lambda: dom_from(1) * dom_width]))
        joined = jnp.concatenate(received, axis=1)
        for k, part in enumerate(around(joined, "gen")):
            places = [
                lambda k=k, i=i: dom_from(i) * dom_width + gen_from(k) * span
                for i in range(2, dom_count)
            ]
            dom_parts.append((part, places))
    else:
        for k, part in enumerate(around(dom_rows, "dom")[1:]):
            dom_parts.append((part, [lambda k=k: dom_from(k + 1) * dom_width]))
    gen_stats = stats(gen_parts, gen_gain, gen_head, wanted, live, dom_count)
    dom_stats = stats(dom_parts, dom_gain, dom_head, wanted, live, dom_count)
    both = jnp.concatenate([gen_stats, dom_stats], axis=1)
    sent = jnp.broadcast_to(both[None], (gen_count,) + both.shape)
    sent = sent.reshape((gen_count * dom_count,) + both.shape[1:])
    gathered = lax.all_to_all(sent, ("gen", "dom"), 0, 0)
    return finish(gathered, doc)


def solution(mesh):
    in_specs = (
        P(("dp", "dom"), "gen"),
        P("dp"),
        P(("dp", "gen", "dom"), None),
        P(("dp", "gen"), "dom"),
        P("dp"),
        P(("dp", "gen", "dom"), None),
        P("dp"),
        P("dp"),
    )
    out_specs = (P(("dp", "dom")), P(("dp", "dom")))
    return jax.shard_map(
        per_device, mesh=mesh, in_specs=in_specs, out_specs=out_specs, check_vma=False
    )
```

```python
import functools

import jax
import jax.numpy as jnp
from jax import lax
from jax.experimental import pallas as pl
from jax.experimental.pallas import tpu as pltpu
from jax.sharding import PartitionSpec as P


DOC_PACK = 8
EPS = 1e-05
PORTIONS = (3, 5)
VMEM = pltpu.VMEM


def whole(memory_space=VMEM):
    return pl.BlockSpec(memory_space=memory_space)


def origin(axis, index, k, count):
    if axis == "gen" and count & (count - 1) == 0:
        return index ^ k
    return (index - k + count) % count


def portions(width):
    edges, done = [0], 0
    for portion in PORTIONS[:-1]:
        done += portion
        edge = max(width * done // sum(PORTIONS) // 128 * 128, edges[-1] + 128)
        edges.append(edge)
    edges.append(width)
    return list(zip(edges, edges[1:]))


def moved(block, axis, k):
    count = lax.axis_size(axis)
    pairs = [(origin(axis, i, k, count), i) for i in range(count)]
    return lax.ppermute(block, axis, pairs)


def around(block, axis):
    return [block] + [moved(block, axis, k) for k in range(1, lax.axis_size(axis))]


def pack_extents(doc):
    live = jnp.where(doc >= 0, 1.0, 0.0)
    counts = jnp.sum(live, axis=1, keepdims=True)
    ahead = jnp.zeros((1, 1), jnp.float32)
    extents = []
    for p in range(doc.shape[0]):
        count = counts[p : p + 1, :]
        extents.append((count, ahead))
        ahead = ahead + count
    return extents


def slot_mask(extent, slots, rows):
    count, ahead = extent
    slot = lax.broadcasted_iota(jnp.int32, (slots, rows), 0).astype(jnp.float32)
    row = lax.broadcasted_iota(jnp.int32, (slots, rows), 1).astype(jnp.float32)
    return (slot - ahead == row) & (row < count)


def prepare_kernel(vocab, *refs):
    doc_ref, target_ref, gen_gain_ref, dom_gain_ref, rows_ref = refs[:5]
    doc_out, live_ref, wanted_ref, gen_gain_out, dom_gain_out, rows_out = refs[5:]
    doc_out[...] = doc_ref[...]
    gen_gain_out[...] = gen_gain_ref[...]
    dom_gain_out[...] = dom_gain_ref[...]
    rows_out[...] = rows_ref[...]
    packs, rows = doc_ref.shape
    slots = live_ref.shape[0]
    extents = pack_extents(doc_ref[...])
    device = lax.axis_index("gen") * lax.axis_size("dom") + lax.axis_index("dom")
    ids = jnp.zeros((slots, 1), jnp.float32)
    for p in range(packs):
        mask = slot_mask(extents[p], slots, rows)
        live_ref[:, p * rows : (p + 1) * rows] = jnp.where(mask, 1.0, 0.0).astype(jnp.bfloat16)
        row = (target_ref[p : p + 1, :] - device * vocab).astype(jnp.float32)
        ids = ids + jnp.sum(jnp.where(mask, row, 0.0), axis=1, keepdims=True)
    wanted_ref[...] = jnp.broadcast_to(ids.astype(jnp.int32), wanted_ref.shape)


def prepare(doc, target, gen_gain, dom_gain, rows_in, slots, vocab):
    like = lambda x: jax.ShapeDtypeStruct(x.shape, x.dtype)
    return pl.pallas_call(
        functools.partial(prepare_kernel, vocab),
        out_shape=(
            like(doc),
            jax.ShapeDtypeStruct((slots, doc.size), jnp.bfloat16),
            jax.ShapeDtypeStruct((slots, 128), jnp.int32),
            like(gen_gain),
            like(dom_gain),
            like(rows_in),
        ),
        in_specs=[whole()] * 5,
        out_specs=[whole()] * 6,
        compiler_params=pltpu.CompilerParams(vmem_limit_bytes=8 * 1024 * 1024),
    )(doc, target, gen_gain, dom_gain, rows_in)


def compact_kernel(pack_axis, spans, live_ref, *refs):
    part_refs = refs[:-2] if spans else refs[:-1]
    out_ref = refs[len(part_refs)]
    rows = part_refs[0].shape[0]
    mine = lax.axis_index(pack_axis)
    total = None
    for k, part_ref in enumerate(part_refs):
        pack = origin(pack_axis, mine, k, len(part_refs))
        live = live_ref[:, pl.ds(pl.multiple_of(pack * rows, rows), rows)]
        piece = jnp.dot(live, part_ref[...], preferred_element_type=jnp.float32)
        total = piece if total is None else total + piece
    out_ref[...] = total.astype(jnp.bfloat16)
    if spans:
        span_ref = refs[-1]
        width = span_ref.shape[1]
        start = pl.multiple_of(mine * width, width)
        span_ref[...] = out_ref[:, pl.ds(start, width)]


def compact(parts, live, pack_axis, spans=0):
    width = parts[0].shape[1]
    slots = live.shape[0]
    out_shape = [jax.ShapeDtypeStruct((slots, width), jnp.bfloat16)]
    if spans:
        out_shape.append(jax.ShapeDtypeStruct((slots, width // spans), jnp.bfloat16))
    return pl.pallas_call(
        functools.partial(compact_kernel, pack_axis, spans),
        out_shape=out_shape,
        in_specs=[whole()] * (1 + len(parts)),
        out_specs=[whole()] * len(out_shape),
        compiler_params=pltpu.CompilerParams(vmem_limit_bytes=16 * 1024 * 1024),
        cost_estimate=pl.CostEstimate(
            flops=2 * width * live.size,
            bytes_accessed=2 * width * (live.shape[1] + slots),
            transcendentals=0,
        ),
    )(live, *parts)


def tally(logits, wanted, top, total, picked):
    lanes = top.shape[1]
    groups = [logits[:, at : at + lanes] for at in range(0, logits.shape[1], lanes)]
    former = top[...]
    highest = functools.reduce(jnp.maximum, groups, former)
    lane = lax.broadcasted_iota(jnp.int32, former.shape, 1)
    away = wanted - lane
    latest = total[...] * jnp.exp(former - highest)
    hit = picked[...]
    for k, group in enumerate(groups):
        latest = latest + jnp.exp(group - highest)
        hit = jnp.where(away == k * lanes, group, hit)
    top[...] = highest
    total[...] = latest
    picked[...] = hit


def summed_up(top, total, picked):
    highest = jnp.max(top[...], axis=1, keepdims=True)
    everything = jnp.sum(total[...] * jnp.exp(top[...] - highest), axis=1, keepdims=True)
    return highest + jnp.log(everything), jnp.sum(picked[...], axis=1, keepdims=True)


def stats_kernel(pieces, buffers, wanted_ref, live_ref, gain_ref, head_ref, *refs):
    part_count = pieces[-1][0] + 1
    part_refs = refs[:part_count]
    out_ref, normed, tiles, sems, top, total, picked = refs[part_count:]
    slots, width = normed.shape
    tile = tiles.shape[1]
    packs, _, rows = out_ref.shape
    j = pl.program_id(0)
    steps = pl.num_programs(0)

    def copy(step):
        slot = lax.rem(step, buffers)
        return pltpu.make_async_copy(
            head_ref.at[pl.ds(pl.multiple_of(step * tile, tile), tile), :],
            tiles.at[slot],
            sems.at[slot],
        )

    @pl.when(j == 0)
    def _():
        copy(0).start()
        for step in range(1, buffers - 1):
            pl.when(step < steps)(lambda: copy(step).start())

    @pl.when(j + buffers - 1 < steps)
    def _():
        copy(j + buffers - 1).start()

    @pl.when(j == 0)
    def _():
        squares = jnp.zeros((slots, 128), jnp.float32)
        for part_ref in part_refs:
            for start in range(0, part_ref.shape[1], 128):
                values = part_ref[:, start : start + 128].astype(jnp.float32)
                squares = squares + values * values
        sums = jnp.sum(squares, axis=1, keepdims=True)
        scale = lax.rsqrt(sums / width + EPS)
        for part, start, extent, place in pieces:
            at = pl.ds(pl.multiple_of(place(), 128), extent)
            values = part_refs[part][:, start : start + extent].astype(jnp.float32)
            normed[:, at] = (values * scale * gain_ref[:, at]).astype(jnp.bfloat16)
        top[...] = jnp.full(top.shape, -jnp.inf, jnp.float32)
        total[...] = jnp.zeros(total.shape, jnp.float32)
        picked[...] = jnp.zeros(picked.shape, jnp.float32)

    copy(j).wait()
    logits = lax.dot_general(
        normed[...],
        tiles[lax.rem(j, buffers)],
        (((1,), (1,)), ((), ())),
        preferred_element_type=jnp.float32,
    )
    tally(logits, wanted_ref[...] - j * tile, top, total, picked)

    @pl.when(j == steps - 1)
    def _():
        log_total, logit = summed_up(top, total, picked)
        for p in range(packs):
            mask = live_ref[:, p * rows : (p + 1) * rows].astype(jnp.float32) > 0.5
            out_ref[p, 0:1, :] = jnp.sum(jnp.where(mask, log_total, 0.0), axis=0, keepdims=True)
            out_ref[p, 1:2, :] = jnp.sum(jnp.where(mask, logit, 0.0), axis=0, keepdims=True)


def stats(parts, gain, head, wanted, live, packs):
    slots = parts[0][0].shape[0]
    vocab, width = head.shape
    rows = live.shape[1] // packs
    tile = min(512, vocab)
    buffers = 3
    pieces = []
    for number, (array, places) in enumerate(parts):
        extent = array.shape[1] // len(places)
        for k, place in enumerate(places):
            pieces.append((number, k * extent, extent, place))
    column = VMEM((slots, 128), jnp.float32)
    return pl.pallas_call(
        functools.partial(stats_kernel, tuple(pieces), buffers),
        grid=(vocab // tile,),
        in_specs=[whole(), whole(), whole(), whole(pl.ANY)] + [whole() for _ in parts],
        out_specs=whole(),
        out_shape=jax.ShapeDtypeStruct((packs, 2, rows), jnp.float32),
        scratch_shapes=[
            VMEM((slots, width), jnp.bfloat16),
            VMEM((buffers, tile, width), jnp.bfloat16),
            pltpu.SemaphoreType.DMA((buffers,)),
            column,
            column,
            column,
        ],
        compiler_params=pltpu.CompilerParams(vmem_limit_bytes=32 * 1024 * 1024),
        cost_estimate=pl.CostEstimate(
            flops=2 * slots * width * vocab,
            bytes_accessed=2 * width * (vocab + slots),
            transcendentals=slots * vocab,
        ),
    )(wanted, live, gain, head, *[array for array, _ in parts])


def finish_kernel(doc_ref, all_ref, token_ref, score_ref):
    pack = lax.axis_index("dom")
    members = all_ref.shape[0]
    both = all_ref[...]

    def log_prob(at):
        logs = [both[i, at : at + 1, :] for i in range(members)]
        highest = functools.reduce(jnp.maximum, logs)
        summed = functools.reduce(jnp.add, [jnp.exp(one - highest) for one in logs])
        logit = functools.reduce(jnp.add, [both[i, at + 1 : at + 2, :] for i in range(members)])
        return logit - (highest + jnp.log(summed))

    ids = doc_ref[pl.ds(pack, 1), :]
    diff = jnp.where(ids >= 0, log_prob(2) - log_prob(0), 0.0)
    token_ref[...] = diff
    rows = ids.shape[1]
    number = lax.broadcasted_iota(jnp.int32, (DOC_PACK, rows), 0) + pack * DOC_PACK
    mine = number == ids
    sums = jnp.sum(jnp.where(mine, diff, 0.0), axis=1, keepdims=True)
    counts = jnp.sum(jnp.where(mine, 1.0, 0.0), axis=1, keepdims=True)
    score = sums / counts
    row = lax.broadcasted_iota(jnp.int32, (DOC_PACK, DOC_PACK), 0)
    column = lax.broadcasted_iota(jnp.int32, (DOC_PACK, DOC_PACK), 1)
    score_ref[...] = jnp.sum(jnp.where(row == column, score, 0.0), axis=0, keepdims=True)


def finish(gathered, doc):
    rows = doc.shape[1]
    token, score = pl.pallas_call(
        finish_kernel,
        out_shape=(
            jax.ShapeDtypeStruct((1, rows), jnp.float32),
            jax.ShapeDtypeStruct((1, DOC_PACK), jnp.float32),
        ),
        in_specs=[whole(), whole()],
        out_specs=(whole(), whole()),
        compiler_params=pltpu.CompilerParams(vmem_limit_bytes=8 * 1024 * 1024),
    )(doc, gathered)
    return token.reshape(rows), score.reshape(DOC_PACK)


def per_device(gen_hidden, gen_gain, gen_head, dom_hidden, dom_gain, dom_head, targets, doc_ids):
    rows = gen_hidden.shape[0]
    gen_count = lax.axis_size("gen")
    dom_count = lax.axis_size("dom")
    doc = doc_ids.reshape(dom_count, rows)
    target = targets.reshape(dom_count, rows)
    slots = dom_count // 2 * (rows + DOC_PACK)
    width = gen_head.shape[1]
    block_width = gen_hidden.shape[1]
    cuts = portions(block_width)
    dom_width = dom_hidden.shape[1]
    spans = gen_count if dom_width % (gen_count * 128) == 0 else 0
    gen_from = lambda k: origin("gen", lax.axis_index("gen"), k, gen_count)
    dom_from = lambda k: origin("dom", lax.axis_index("dom"), k, dom_count)
    doc, live, wanted, gen_gain, dom_gain, dom_own = prepare(
        doc, target, gen_gain.reshape(1, width), dom_gain.reshape(1, width), dom_hidden,
        slots, gen_head.shape[0],
    )
    gen_first = [around(gen_hidden[:, start:stop], "dom") for start, stop in cuts]
    dom_first = around(dom_hidden, "gen")
    gen_parts = []
    for h, (start, _) in enumerate(cuts):
        (rows_in,) = compact(gen_first[h], live, "dom")
        for k, part in enumerate(around(rows_in, "gen")):
            place = lambda k=k, start=start: gen_from(k) * block_width + start
            gen_parts.append((part, [place]))
    dom_rows, *dom_span = compact([dom_own] + dom_first[1:], live, "gen", spans)
    dom_parts = [(dom_rows, [lambda: dom_from(0) * dom_width])]
    if spans:
        span = dom_width // spans
        received = [moved(dom_span[0], "dom", k) for k in range(2, dom_count)]
        near = moved(dom_rows, "dom", 1)
        dom_parts.append((near, [lambda: dom_from(1) * dom_width]))
        joined = jnp.concatenate(received, axis=1)
        for k, part in enumerate(around(joined, "gen")):
            places = [
                lambda k=k, i=i: dom_from(i) * dom_width + gen_from(k) * span
                for i in range(2, dom_count)
            ]
            dom_parts.append((part, places))
    else:
        for k, part in enumerate(around(dom_rows, "dom")[1:]):
            dom_parts.append((part, [lambda k=k: dom_from(k + 1) * dom_width]))
    gen_stats = stats(gen_parts, gen_gain, gen_head, wanted, live, dom_count)
    dom_stats = stats(dom_parts, dom_gain, dom_head, wanted, live, dom_count)
    both = jnp.concatenate([gen_stats, dom_stats], axis=1)
    sent = jnp.broadcast_to(both[None], (gen_count,) + both.shape)
    sent = sent.reshape((gen_count * dom_count,) + both.shape[1:])
    gathered = lax.all_to_all(sent, ("gen", "dom"), 0, 0)
    return finish(gathered, doc)


def solution(mesh):
    in_specs = (
        P(("dp", "dom"), "gen"),
        P("dp"),
        P(("dp", "gen", "dom"), None),
        P(("dp", "gen"), "dom"),
        P("dp"),
        P(("dp", "gen", "dom"), None),
        P("dp"),
        P("dp"),
    )
    out_specs = (P(("dp", "dom")), P(("dp", "dom")))
    return jax.shard_map(
        per_device, mesh=mesh, in_specs=in_specs, out_specs=out_specs, check_vma=False
    )
```
